32 devices in a mesh: groups: 2 (over x), ctx: 8 (over z, y), exp: 2 (over core).
Axes of the slice: x: 2, y: 2, z: 4, core: 2. Of those that a mesh axis runs over, the one named last changes fastest.
Arguments:
- query_states: bfloat16 [1024, 3072], P(('groups', 'ctx'), 'exp'), parts along dimension 0, may hold values from -5 to 5
- key_states: bfloat16 [1024, 512], P(('groups', 'ctx'), 'exp'), parts along dimension 0, may hold values from -5 to 5
- value_states: bfloat16 [1024, 512], P(('groups', 'ctx'), 'exp'), parts along dimension 0, may hold values from -6 to 6
- residual: bfloat16 [1024, 3072], P(('groups', 'ctx'), 'exp'), parts along dimension 0, may hold values from -2 to 2
- norm_gain: float32 [3072], replicated, may hold values from 0.1 to 1.9
- expert_ids: int32 [1024, 2], P(('groups', 'ctx')), parts along dimension 0, may hold values from 0 to 7, all different within a row; in each aligned block of 32 rows (0 to 31, 32 to 63, ...) at most 12 rows name the same one
- route_weights: float32 [1024, 2], P(('groups', 'ctx')), parts along dimension 0, may hold values from 0.1 to 1
- w_gate: bfloat16 [3072, 16384], P(None, ('ctx', 'exp')), may hold values from -0.109375 to 0.109375
- w_down: bfloat16 [16384, 3072], P(('ctx', 'exp')), may hold values from -0.125 to 0.125
Outputs:
- mixed: bfloat16 [1024, 3072], P(('groups', 'ctx'), 'exp'), parts along dimension 0
The draws below stay inside these ranges and needn't reach their ends.
There are 2 independent parts, one for each index of `groups`. The reference program is written for one: setup_inputs(seed, part) draws one part's arguments, and reference() takes and returns one part's arrays. A program takes and returns all parts, laid end to end along the dimension named above; an argument that names none is the same for every part. Nothing has to cross between parts.
Inputs may be any that keep to these rules, and one draw needn't show every extreme that they name: `expert_ids`: each token names 2 different experts. In each aligned block of 32 tokens, at most 12 tokens name the same expert.
All inputs are finite; a program needn't handle non-finite values.
Results may differ from the reference program's by a relative error of at most 0.012.
Values may be sent and summed in bfloat16 or wider, within the bound.
A program may use at most 64 MiB of HBM per device.

```python
import math
import jax
import jax.numpy as jnp
import numpy as np
from jax import lax

D = 3072
HEADS = 24
KV_HEADS = 4
HEAD_DIM = 128
EXPERTS = 8
TOP = 2
HALF_BLOCK = 32
HALF_CAP = 12
CAP = 24
TOKENS = 512
FF = 2048
N_CTX = 8


def drawn_pair(key):
    base_key = jax.random.fold_in(key, 7)
    subkeys = jax.random.split(base_key, 2)
    query_shape = (TOKENS, HEADS * HEAD_DIM)
    key_shape = (TOKENS, KV_HEADS * HEAD_DIM)
    queries = jax.random.truncated_normal(subkeys[0], -5.0, 5.0, query_shape, jnp.float32)
    keys_drawn = jax.random.truncated_normal(subkeys[1], -5.0, 5.0, key_shape, jnp.float32)
    return (queries, keys_drawn)


def draw_query_states(key, part):
    return drawn_pair(key)[0].astype(jnp.bfloat16)


def draw_key_states(key, part):
    return drawn_pair(key)[1].astype(jnp.bfloat16)


def levels(key, extent, cuts, least, high):
    gain = 1.0
    for dim, parts in cuts:
        steps = jax.random.uniform(jax.random.fold_in(jax.random.fold_in(key, 6), dim), (parts,), jnp.float32, least / len(cuts), high / len(cuts))
        gain = gain * jnp.repeat(jnp.exp(steps), extent[dim] // parts).reshape((-1,) + (1,) * (len(extent) - 1 - dim))
    return gain


def shared_out(rng, own, number, rows, amount, top, limit, lean):
    order = jax.random.permutation(rng, amount)
    heavy_load, common = portions_of(amount, rows * top, limit, lean, True), portions_of(amount, rows * top, limit, lean, False)
    places = jnp.arange(amount)

    def named(lengths, offset_by):
        used = int((lengths > 0).sum())
        fixed = max(1, used // 4)
        shifted = fixed + (places - fixed + offset_by * (used - fixed)) % max(1, amount - fixed)
        return jnp.zeros((amount,), jnp.int32).at[order[jnp.where(places < fixed, places, shifted)]].set(jnp.asarray(lengths, jnp.int32))

    lengths = jnp.where(number % 4 == 0, named(heavy_load, number // 4), named(common, number - number // 4 - 1))
    mixed = jax.random.permutation(jax.random.fold_in(own, 3), amount)
    source_of, receiver = mixed[0:amount // 2 * 2:2], mixed[1:amount // 2 * 2:2]
    room = jnp.minimum(lengths[source_of] - 1, limit - lengths[receiver]) // 2
    room = jnp.where((source_of == order[0]) | (receiver == order[0]) | (lengths[receiver] == 0), 0, jnp.maximum(room, 0))
    shifted = jax.random.randint(jax.random.fold_in(own, 4), (amount // 2,), 0, 1 << 20) % (room + 1)
    lengths = lengths.at[source_of].add(-shifted).at[receiver].add(shifted)
    items = jnp.searchsorted(jnp.cumsum(lengths), jnp.arange(rows * top), side="right").astype(jnp.int32)
    table = items.reshape(top, rows).T
    table = table[jax.random.permutation(jax.random.fold_in(own, 1), rows)]
    offset_by = jax.random.randint(jax.random.fold_in(own, 2), (rows, 1), 0, top)
    return jnp.take_along_axis(table, (jnp.arange(top)[None, :] + offset_by) % top, axis=1)


def portions_of(number_of, total, most, lean, full):
    portions = [(1 << 20) // math.isqrt(standing ** lean) + 1 for standing in range(1, number_of + 1)]
    largest = most if full else min(most, max(-(-total // number_of), total * portions[0] // sum(portions)))
    least = 1 if total - largest >= number_of - 1 else 0
    counts, rest = [largest] + [least] * (number_of - 1), total - largest - least * (number_of - 1)
    while rest > 0:
        free = [i for i in range(1, number_of) if counts[i] < largest] or [i for i in range(1, number_of) if counts[i] < most]
        mass, left = sum([portions[i] for i in free]), rest
        for i in free:
            more = min(most - counts[i], max(1, left * portions[i] // mass), rest)
            counts[i] = counts[i] + more
            rest = rest - more
    return np.array(counts)


def gaussian(own_key, extent, spread, most, shards=(), kind=jnp.bfloat16):
    result = jax.random.normal(own_key, extent, jnp.float32) * spread
    if len(shards) > 0:
        result = levels(own_key, extent, shards, -0.22, 0.18) * result
    return jnp.clip(result, min=-most, max=most).astype(kind)


def setup_inputs(seed: int = 0, part: int = 0) -> dict:
    keys = jax.random.split(jax.random.key(seed), 10)
    part_splits = jax.random.split(jax.random.fold_in(keys[9], part), 10)
    query_states = draw_query_states(jax.random.fold_in(jax.random.fold_in(keys[9], part), 71), part)
    key_states = draw_key_states(jax.random.fold_in(jax.random.fold_in(keys[9], part), 71), part)
    value_states = gaussian(part_splits[2], (TOKENS, KV_HEADS * HEAD_DIM), 1.0, 6.0, ((0, 8), (1, 2)))
    residual = gaussian(part_splits[3], (TOKENS, D), 0.3, 2.0, ((0, 8), (1, 2)))
    norm_gain = jnp.clip(1.0 + 0.18 * jax.random.normal(keys[4], (D,), jnp.float32), 0.1, 1.9)
    expert_ids_keys = jax.random.split(jax.random.fold_in(part_splits[5], 1), TOKENS // HALF_BLOCK)
    expert_ids_turns = jax.random.permutation(jax.random.fold_in(part_splits[5], 3), TOKENS // HALF_BLOCK)
    expert_ids = jax.vmap(lambda own, number: shared_out(jax.random.fold_in(part_splits[5], 2), own, number, HALF_BLOCK, EXPERTS, TOP, HALF_CAP, 2))(expert_ids_keys, expert_ids_turns).reshape((TOKENS, TOP))
    route_weights = jnp.clip(0.1 + 0.9 * jax.random.uniform(part_splits[6], (TOKENS, TOP), jnp.float32) ** levels(part_splits[6], (TOKENS, TOP), ((0, 8),), -0.2, 0.2), 0.1, 1.0)
    w_gate = gaussian(keys[7], (D, EXPERTS * FF), D ** -0.5, 0.109375, ((1, 16),))
    w_down = gaussian(keys[8], (EXPERTS * FF, D), FF ** -0.5, 0.125, ((0, 16),))
    return dict(query_states=query_states, key_states=key_states, value_states=value_states, residual=residual, norm_gain=norm_gain, expert_ids=expert_ids, route_weights=route_weights, w_gate=w_gate, w_down=w_down)


def reference(query_states, key_states, value_states, residual, norm_gain, expert_ids, route_weights, w_gate, w_down):
    per_group = HEADS // KV_HEADS
    tok_count = query_states.shape[0]
    query_heads = query_states.reshape(tok_count, KV_HEADS, per_group, HEAD_DIM).transpose(1, 0, 2, 3)
    key_heads = key_states.reshape(tok_count, KV_HEADS, HEAD_DIM).transpose(1, 0, 2)
    value_heads = value_states.reshape(tok_count, KV_HEADS, HEAD_DIM).transpose(1, 0, 2)
    position = jnp.arange(tok_count, dtype=jnp.int32)
    allowed = position[None, :] <= position[:, None]
    scaling = HEAD_DIM ** (-0.5)

    def one_head(operands):
        query_block, key_block, value_block = operands
        scores = jnp.einsum('qjd,kd->jqk', query_block.astype(jnp.float32), key_block.astype(jnp.float32)) * scaling
        row_max = lax.optimization_barrier(jnp.max(jnp.where(allowed[None], scores, -jnp.inf), axis=-1, keepdims=True))
        expo_terms = jnp.where(allowed[None], jnp.exp(scores - row_max), 0.0)
        totals = lax.optimization_barrier(jnp.sum(expo_terms, axis=-1))
        rounded = expo_terms.astype(jnp.bfloat16).astype(jnp.float32)
        weighted = jnp.einsum('jqk,kd->jqd', rounded, value_block.astype(jnp.float32))
        return (weighted / totals[..., None]).transpose(1, 0, 2)
    per_head = lax.map(one_head, (query_heads, key_heads, value_heads))
    attended = per_head.transpose(1, 0, 2, 3).reshape(tok_count, D)
    hidden = (residual.astype(jnp.float32) + attended).astype(jnp.bfloat16)
    hidden_float = hidden.astype(jnp.float32)
    mean_sq = lax.optimization_barrier(jnp.mean(jnp.square(hidden_float), axis=-1, keepdims=True))
    normed = (hidden_float * lax.rsqrt(mean_sq + 1e-05) * norm_gain.astype(jnp.float32)[None, :]).astype(jnp.bfloat16)
    mixed_sum = jnp.zeros((tok_count, D), jnp.float32)
    row_limit = N_CTX * CAP
    for expert in range(EXPERTS):
        hit_table = (expert_ids == expert).astype(jnp.int32)
        chosen = lax.optimization_barrier(jnp.sum(hit_table, axis=1))
        weight = lax.optimization_barrier(jnp.sum(route_weights * hit_table.astype(route_weights.dtype), axis=1))
        row_order = jnp.argsort(1 - chosen, stable=True)[:row_limit]
        rows = normed[row_order]
        gate_act = jax.nn.silu(jnp.dot(rows, w_gate[:, expert * FF:(expert + 1) * FF], preferred_element_type=jnp.float32)).astype(jnp.bfloat16)
        partial_value = jnp.dot(gate_act, w_down[expert * FF:(expert + 1) * FF], preferred_element_type=jnp.float32)
        mixed_sum = mixed_sum.at[row_order].add(partial_value * weight[row_order][:, None])
    return (hidden_float + mixed_sum).astype(jnp.bfloat16)
```

```python
import functools

import jax
import jax.numpy as jnp
from jax import lax
from jax.experimental import pallas as pl
from jax.experimental.pallas import tpu as pltpu
from jax.sharding import PartitionSpec as P

HEAD_DIM = 128
EXPERTS = 8
HALF_CAP = 12
CAP = 2 * HALF_CAP
CHUNK = 512
MESH = pl.DeviceIdType.MESH
F32 = jnp.float32
BF16 = jnp.bfloat16


def kernel(
    n,
    q_ref, k_ref, v_ref, res_ref, gain_ref, ids_ref, rw_ref, wg_hbm, wd_hbm,
    out_ref,
    kbuf, vbuf, wg, wd, hid, place, comb, sq_send, sq_recv,
    send_buf, recv_own, recv_sib, lhs_own, lhs_sib, acc, act,
    psend, precv, rsend, rrecv,
    w_sem, kv_send, kv_recv, sq_sem, disp_send, disp_recv, sib_send, sib_recv,
    p_send, p_recv, r_send, r_recv,
):
    me = lax.axis_index("ctx")
    x = lax.axis_index("exp")
    sib = 1 - x
    toks = q_ref.shape[0]
    half_feat = q_ref.shape[1]
    kv_local = k_ref.shape[1] // HEAD_DIM
    per_group = half_feat // HEAD_DIM // kv_local
    spread = n // EXPERTS
    slots = EXPERTS * CAP
    chunks = half_feat // CHUNK
    nz = n // 2
    rows = n * CAP
    ff = wg.shape[1]

    wg_copy = pltpu.make_async_copy(wg_hbm, wg, w_sem.at[0])
    wd_copy = pltpu.make_async_copy(wd_hbm, wd, w_sem.at[1])
    wg_copy.start()
    wd_copy.start()

    barrier = pltpu.get_barrier_semaphore()
    for d in range(1, n):
        pl.semaphore_signal(
            barrier, inc=1, device_id={"ctx": lax.rem(me + d, n)}, device_id_type=MESH
        )
    pl.semaphore_signal(barrier, inc=1, device_id={"exp": sib}, device_id_type=MESH)
    pl.semaphore_wait(barrier, n)

    parity = lax.rem(me, 2)
    level = lax.div(me, 2)
    partner = me + 1 - 2 * parity
    bufs = (kbuf, vbuf)

    def kv_copy(i, src, block, dst, slot):
        return pltpu.make_async_remote_copy(
            src_ref=src,
            dst_ref=bufs[i].at[block],
            send_sem=kv_send.at[i, slot],
            recv_sem=kv_recv.at[i, block],
            device_id={"ctx": dst},
            device_id_type=MESH,
        )

    def own_copies(dst, slot):
        return [kv_copy(i, (k_ref, v_ref)[i], me, dst, slot) for i in range(2)]

    def relay_copies(block, slot):
        return [kv_copy(i, bufs[i].at[block], block, partner, slot) for i in range(2)]

    @pl.when(parity == 0)
    def _():
        for c in own_copies(partner, 0):
            c.start()

    for dz in range(1, nz):
        @pl.when(level + dz < nz)
        def _():
            for c in own_copies(me + 2 * dz, dz):
                c.start()

    kbuf[me] = k_ref[...]
    vbuf[me] = v_ref[...]
    for b in range(n):
        @pl.when(b > me)
        def _():
            kbuf[b] = jnp.zeros(k_ref.shape, BF16)
            vbuf[b] = jnp.zeros(v_ref.shape, BF16)

    slot = lax.broadcasted_iota(jnp.int32, (toks, slots), 1)
    expert = jnp.zeros((toks, slots), jnp.int32)
    for e in range(1, EXPERTS):
        expert = expert + (slot >= e * CAP).astype(jnp.int32)
    pos = slot - expert * CAP
    token = lax.broadcasted_iota(jnp.int32, (toks, slots), 0)
    block_len = toks // 2
    in_second = (token >= block_len).astype(jnp.int32)
    ids = ids_ref[...]
    rw = rw_ref[...]
    first = jnp.where(ids[:, 0:1] == expert, 1.0, 0.0)
    second = jnp.where(ids[:, 1:2] == expert, 1.0, 0.0)
    chosen = first + second
    t_row = lax.broadcasted_iota(jnp.int32, (toks, toks), 0)
    t_col = lax.broadcasted_iota(jnp.int32, (toks, toks), 1)
    same = (t_row >= block_len) == (t_col >= block_len)
    lower = jnp.where(same & (t_col < t_row), 1.0, 0.0).astype(BF16)
    rank = jnp.dot(lower, chosen.astype(BF16), preferred_element_type=F32)
    wanted = (pos - in_second * HALF_CAP).astype(F32)
    placing = jnp.where(rank == wanted, chosen, 0.0)
    place[...] = placing
    weight = placing * (first * rw[:, 0:1] + second * rw[:, 1:2])
    high = weight.astype(BF16)
    comb[0:toks, :] = high
    comb[toks:, :] = (weight - high.astype(F32)).astype(BF16)

    for dz in range(1, nz):
        @pl.when(level - dz >= 0)
        def _():
            block = me - 2 * dz
            for c in relay_copies(block, nz + dz - 1):
                c.wait_recv()
                c.start()
    for j in range(nz):
        block = 2 * j + 1 - parity

        @pl.when(block < me)
        def _():
            for c in relay_copies(block, 0):
                c.wait_recv()

    keys = n * toks
    q_pos = me * toks + lax.broadcasted_iota(jnp.int32, (toks, keys), 0)
    k_pos = lax.broadcasted_iota(jnp.int32, (toks, keys), 1)
    bias = jnp.where(k_pos <= q_pos, 0.0, -1e30)
    bias = jnp.concatenate([bias] * per_group, axis=0)
    scaling = HEAD_DIM ** (-0.5)
    squares = jnp.zeros((toks, 1), F32)
    for g in range(kv_local):
        head = slice(g * HEAD_DIM, (g + 1) * HEAD_DIM)
        base = g * per_group * HEAD_DIM
        qs = jnp.concatenate(
            [
                q_ref[:, base + j * HEAD_DIM : base + (j + 1) * HEAD_DIM]
                for j in range(per_group)
            ],
            axis=0,
        )
        ks = kbuf[:, :, head].reshape(keys, HEAD_DIM)
        vs = vbuf[:, :, head].reshape(keys, HEAD_DIM)
        s = lax.dot_general(qs, ks, (((1,), (1,)), ((), ())), preferred_element_type=F32)
        s = s * scaling + bias
        m = jnp.max(s, axis=1, keepdims=True)
        p = jnp.exp(s - m)
        total = jnp.sum(p, axis=1, keepdims=True)
        att = jnp.dot(p.astype(BF16), vs, preferred_element_type=F32) / total
        for j in range(per_group):
            cols = slice(base + j * HEAD_DIM, base + (j + 1) * HEAD_DIM)
            h = (res_ref[:, cols].astype(F32) + att[j * toks : (j + 1) * toks]).astype(BF16)
            hid[:, cols] = h
            squares = squares + jnp.sum(jnp.square(h.astype(F32)), axis=1, keepdims=True)

    sq_send[...] = jnp.broadcast_to(squares, sq_send.shape)
    sq_copy = pltpu.make_async_remote_copy(
        src_ref=sq_send, dst_ref=sq_recv, send_sem=sq_sem.at[0], recv_sem=sq_sem.at[1],
        device_id={"exp": sib}, device_id_type=MESH,
    )
    sq_copy.start()
    my_feat = pl.multiple_of(x * half_feat, half_feat)
    sib_feat = pl.multiple_of(sib * half_feat, half_feat)
    gain = gain_ref[:, pl.ds(my_feat, half_feat)]
    scaled = hid[...].astype(F32)
    sq_copy.wait()
    inv = lax.rsqrt((squares + sq_recv[:, 0:1]) / (2 * half_feat) + 1e-05)
    normed = (scaled * inv * gain).astype(BF16)

    sent = lax.dot_general(
        place[...].astype(BF16), normed, (((0,), (0,)), ((), ())), preferred_element_type=F32
    )
    send_buf[...] = sent.reshape(EXPERTS, CAP, half_feat).astype(BF16)
    my_expert = lax.div(me, spread)

    def disp_copy(dst, block, src_expert, slot):
        return pltpu.make_async_remote_copy(
            src_ref=send_buf.at[src_expert], dst_ref=recv_own.at[block],
            send_sem=disp_send.at[slot], recv_sem=disp_recv.at[block],
            device_id={"ctx": dst}, device_id_type=MESH,
        )

    def sib_copy(src, block):
        return pltpu.make_async_remote_copy(
            src_ref=src, dst_ref=recv_sib.at[block],
            send_sem=sib_send.at[block], recv_sem=sib_recv.at[block],
            device_id={"exp": sib}, device_id_type=MESH,
        )

    for d in range(1, n):
        dst = lax.rem(me + d, n)
        disp_copy(dst, me, lax.div(dst, spread), d).start()
    sib_copy(send_buf.at[my_expert], me).start()
    recv_own[me] = send_buf[my_expert]
    for d in range(1, n):
        src = lax.rem(me - d + n, n)
        disp_copy(src, src, my_expert, d).wait_recv()
        sib_copy(recv_own.at[src], src).start()

    lhs_own[...] = recv_own[...].astype(F32).reshape(rows, half_feat).astype(BF16)
    wg_copy.wait()
    for c in range(ff // 256):
        cols = slice(c * 256, (c + 1) * 256)
        acc[:, cols] = jnp.dot(
            lhs_own[...], wg[pl.ds(my_feat, half_feat), cols], preferred_element_type=F32
        )
    for d in range(n):
        sib_copy(send_buf.at[0], lax.rem(me - d + n, n)).wait_recv()
    lhs_sib[...] = recv_sib[...].astype(F32).reshape(rows, half_feat).astype(BF16)
    for c in range(ff // 256):
        cols = slice(c * 256, (c + 1) * 256)
        v = acc[:, cols] + jnp.dot(
            lhs_sib[...], wg[pl.ds(sib_feat, half_feat), cols], preferred_element_type=F32
        )
        act[:, cols] = (v / (1.0 + jnp.exp(-v))).astype(BF16)

    def p_copy(j):
        return pltpu.make_async_remote_copy(
            src_ref=psend.at[j], dst_ref=precv.at[j],
            send_sem=p_send.at[j], recv_sem=p_recv.at[j],
            device_id={"exp": sib}, device_id_type=MESH,
        )

    def r_copy(j, dst, block, slot):
        return pltpu.make_async_remote_copy(
            src_ref=rsend.at[j, dst], dst_ref=rrecv.at[j, block],
            send_sem=r_send.at[j, slot], recv_sem=r_recv.at[j, block],
            device_id={"ctx": dst}, device_id_type=MESH,
        )

    wd_copy.wait()
    for j in range(chunks):
        cols = pl.ds(pl.multiple_of(sib_feat + j * CHUNK, CHUNK), CHUNK)
        y = jnp.dot(act[...], wd[:, cols], preferred_element_type=F32)
        psend[j] = y.reshape(n, CAP, CHUNK).astype(BF16)
        p_copy(j).start()
    for j in range(chunks):
        cols = pl.ds(pl.multiple_of(my_feat + j * CHUNK, CHUNK), CHUNK)
        y = jnp.dot(act[...], wd[:, cols], preferred_element_type=F32)
        p_copy(j).wait_recv()
        rsend[j] = (y.reshape(n, CAP, CHUNK) + precv[j].astype(F32)).astype(BF16)
        for d in range(1, n):
            r_copy(j, lax.rem(me + d, n), me, d).start()
        rrecv[j, me] = rsend[j, me]

    for j in range(chunks):
        for d in range(1, n):
            src = lax.rem(me - d + n, n)
            r_copy(j, src, src, d).wait_recv()
        back = rrecv[j].astype(F32).reshape(EXPERTS, spread, CAP, CHUNK)
        if spread == 1:
            back = back.reshape(slots, CHUNK).astype(BF16)
            both = jnp.dot(comb[...], back, preferred_element_type=F32)
        else:
            back = jnp.sum(back, axis=1).reshape(slots, CHUNK)
            top = back.astype(BF16)
            rest = (back - top.astype(F32)).astype(BF16)
            both = jnp.dot(comb[...], top, preferred_element_type=F32)
            both = both + jnp.dot(comb[...], rest, preferred_element_type=F32)
        cols = slice(j * CHUNK, (j + 1) * CHUNK)
        mixed = hid[:, cols].astype(F32) + both[:toks] + both[toks:]
        out_ref[:, cols] = mixed.astype(BF16)

    @pl.when(parity == 0)
    def _():
        for c in own_copies(partner, 0):
            c.wait_send()

    for dz in range(1, nz):
        @pl.when(level + dz < nz)
        def _():
            for c in own_copies(me + 2 * dz, dz):
                c.wait_send()

        @pl.when(level - dz >= 0)
        def _():
            for c in relay_copies(me - 2 * dz, nz + dz - 1):
                c.wait_send()

    for d in range(1, n):
        dst = lax.rem(me + d, n)
        disp_copy(dst, me, lax.div(dst, spread), d).wait_send()
    for d in range(n):
        sib_copy(send_buf.at[0], lax.rem(me - d + n, n)).wait_send()
    for j in range(chunks):
        p_copy(j).wait_send()
        for d in range(1, n):
            r_copy(j, lax.rem(me + d, n), me, d).wait_send()


def solution(mesh):
    n = mesh.shape["ctx"]

    def body(q, k, v, res, gain, ids, rw, w_gate, w_down):
        toks, half_feat = q.shape
        ff = w_gate.shape[1]
        rows = n * CAP
        slots = EXPERTS * CAP
        chunks = half_feat // CHUNK
        dma = pltpu.SemaphoreType.DMA
        vmem = pl.BlockSpec(memory_space=pltpu.VMEM)
        anyspace = pl.BlockSpec(memory_space=pl.ANY)
        return pl.pallas_call(
            functools.partial(kernel, n),
            out_shape=jax.ShapeDtypeStruct((toks, half_feat), BF16),
            in_specs=[vmem] * 7 + [anyspace] * 2,
            out_specs=vmem,
            scratch_shapes=[
                pltpu.VMEM((n, toks, k.shape[1]), BF16),
                pltpu.VMEM((n, toks, k.shape[1]), BF16),
                pltpu.VMEM(w_gate.shape, BF16),
                pltpu.VMEM(w_down.shape, BF16),
                pltpu.VMEM((toks, half_feat), BF16),
                pltpu.VMEM((toks, slots), F32),
                pltpu.VMEM((2 * toks, slots), BF16),
                pltpu.VMEM((toks, 128), F32),
                pltpu.VMEM((toks, 128), F32),
                pltpu.VMEM((EXPERTS, CAP, half_feat), BF16),
                pltpu.VMEM((n, CAP, half_feat), BF16),
                pltpu.VMEM((n, CAP, half_feat), BF16),
                pltpu.VMEM((rows, half_feat), BF16),
                pltpu.VMEM((rows, half_feat), BF16),
                pltpu.VMEM((rows, ff), F32),
                pltpu.VMEM((rows, ff), BF16),
                pltpu.VMEM((chunks, n, CAP, CHUNK), BF16),
                pltpu.VMEM((chunks, n, CAP, CHUNK), BF16),
                pltpu.VMEM((chunks, n, CAP, CHUNK), BF16),
                pltpu.VMEM((chunks, n, CAP, CHUNK), BF16),
                dma((2,)),
                dma((2, n)),
                dma((2, n)),
                dma((2,)),
                dma((n,)),
                dma((n,)),
                dma((n,)),
                dma((n,)),
                dma((chunks,)),
                dma((chunks,)),
                dma((chunks, n)),
                dma((chunks, n)),
            ],
            compiler_params=pltpu.CompilerParams(
                collective_id=0, has_side_effects=True, vmem_limit_bytes=60 * 1024 * 1024
            ),
        )(q, k, v, res, gain.reshape(1, -1), ids, rw, w_gate, w_down)

    rows_spec = P(("groups", "ctx"), "exp")
    in_specs = (
        rows_spec, rows_spec, rows_spec, rows_spec, P(),
        P(("groups", "ctx"), None), P(("groups", "ctx"), None),
        P(None, ("ctx", "exp")), P(("ctx", "exp"), None),
    )
    return jax.shard_map(
        body, mesh=mesh, in_specs=in_specs, out_specs=rows_spec, check_vma=False
    )
```

```python
import functools

import jax
import jax.numpy as jnp
from jax import lax
from jax.experimental import pallas as pl
from jax.experimental.pallas import tpu as pltpu
from jax.sharding import PartitionSpec as P

HEAD_DIM = 128
EXPERTS = 8
HALF_CAP = 12
CAP = 2 * HALF_CAP
PARTS = (16, 8)
CHUNK = 768
MESH = pl.DeviceIdType.MESH
F32 = jnp.float32
BF16 = jnp.bfloat16


def kernel(
    n,
    q_ref, k_ref, v_ref, res_ref, gain_ref, ids_ref, rw_ref, wg_hbm, wd_hbm,
    hid, branch,
    kbuf, vbuf, wg, wd, place, comb, sq_send, sq_recv,
    send_a, send_b, own_a, own_b, other_a, other_b, acc, act, flat,
    psend_a, psend_b, precv_a, precv_b, rsend_a, rsend_b, rrecv_a, rrecv_b,
    w_sem, kv_send, kv_recv, sq_sem, disp_send, disp_recv, sib_send, sib_recv,
    p_send, p_recv, r_send, r_recv,
):
    send_buf, recv_own, recv_sib = (send_a, send_b), (own_a, own_b), (other_a, other_b)
    psend, precv = (psend_a, psend_b), (precv_a, precv_b)
    rsend, rrecv = (rsend_a, rsend_b), (rrecv_a, rrecv_b)
    me = lax.axis_index("ctx")
    x = lax.axis_index("exp")
    sib = 1 - x
    toks = q_ref.shape[0]
    half_feat = q_ref.shape[1]
    kv_local = k_ref.shape[1] // HEAD_DIM
    per_group = half_feat // HEAD_DIM // kv_local
    spread = n // EXPERTS
    slots = EXPERTS * CAP
    chunks = half_feat // CHUNK
    nz = n // 2
    ff = wg.shape[1]

    def flip(m):
        other, bit = me, 1
        while bit < n:
            if m & bit:
                other = other + bit * (1 - 2 * lax.rem(lax.div(me, bit), 2))
            bit *= 2
        return other

    order = range(1, n)

    wg_copy = pltpu.make_async_copy(wg_hbm, wg, w_sem.at[0])
    wd_copy = pltpu.make_async_copy(wd_hbm, wd, w_sem.at[1])
    wg_copy.start()
    wd_copy.start()

    barrier = pltpu.get_barrier_semaphore()
    for d in range(1, n):
        pl.semaphore_signal(
            barrier, inc=1, device_id={"ctx": lax.rem(me + d, n)}, device_id_type=MESH
        )
    pl.semaphore_signal(barrier, inc=1, device_id={"exp": sib}, device_id_type=MESH)
    pl.semaphore_wait(barrier, n)

    parity = lax.rem(me, 2)
    level = lax.div(me, 2)
    partner = me + 1 - 2 * parity
    bufs = (kbuf, vbuf)

    def kv_copy(i, src, block, dst, slot):
        return pltpu.make_async_remote_copy(
            src_ref=src,
            dst_ref=bufs[i].at[block],
            send_sem=kv_send.at[i, slot],
            recv_sem=kv_recv.at[i, block],
            device_id={"ctx": dst},
            device_id_type=MESH,
        )

    def own_copies(dst, slot):
        return [kv_copy(i, (k_ref, v_ref)[i], me, dst, slot) for i in range(2)]

    def relay_copies(block, slot):
        return [kv_copy(i, bufs[i].at[block], block, partner, slot) for i in range(2)]

    @pl.when(parity == 0)
    def _():
        for c in own_copies(partner, 0):
            c.start()

    for dz in range(1, nz):
        @pl.when(level + dz < nz)
        def _():
            for c in own_copies(me + 2 * dz, dz):
                c.start()

    kbuf[me] = k_ref[...]
    vbuf[me] = v_ref[...]
    for b in range(n):
        @pl.when(b > me)
        def _():
            kbuf[b] = jnp.zeros(k_ref.shape, BF16)
            vbuf[b] = jnp.zeros(v_ref.shape, BF16)

    row = lax.broadcasted_iota(jnp.int32, (slots, toks), 0)
    expert = jnp.zeros((slots, toks), jnp.int32)
    pos = row
    start, first_row = 0, 0
    for size in PARTS:
        for e in range(EXPERTS):
            here = row >= start + e * size
            expert = jnp.where(here, e, expert)
            pos = jnp.where(here, row - (start + e * size) + first_row, pos)
        start, first_row = start + EXPERTS * size, first_row + size
    token = lax.broadcasted_iota(jnp.int32, (slots, toks), 1)
    block_len = toks // 2
    in_second = (token >= block_len).astype(jnp.int32)
    ids = ids_ref[...]
    rw = rw_ref[...]
    first = jnp.where(ids[0:1, :] == expert, 1.0, 0.0)
    second = jnp.where(ids[1:2, :] == expert, 1.0, 0.0)
    chosen = first + second
    t_row = lax.broadcasted_iota(jnp.int32, (toks, toks), 0)
    t_col = lax.broadcasted_iota(jnp.int32, (toks, toks), 1)
    same = (t_row >= block_len) == (t_col >= block_len)
    upper = jnp.where(same & (t_row < t_col), 1.0, 0.0).astype(BF16)
    rank = jnp.dot(chosen.astype(BF16), upper, preferred_element_type=F32)
    wanted = (pos - in_second * HALF_CAP).astype(F32)
    placing = jnp.where(rank == wanted, chosen, 0.0)
    place[...] = placing.astype(BF16)
    weight = placing * (first * rw[0:1, :] + second * rw[1:2, :])
    high = weight.astype(BF16)
    comb[:, 0:toks] = high
    comb[:, toks:] = (weight - high.astype(F32)).astype(BF16)

    for dz in range(1, nz):
        @pl.when(level - dz >= 0)
        def _():
            block = me - 2 * dz
            for c in relay_copies(block, nz + dz - 1):
                c.wait_recv()
                c.start()
    for j in range(nz):
        block = 2 * j + 1 - parity

        @pl.when(block < me)
        def _():
            for c in relay_copies(block, 0):
                c.wait_recv()

    keys = n * toks
    q_pos = me * toks + lax.broadcasted_iota(jnp.int32, (toks, keys), 0)
    k_pos = lax.broadcasted_iota(jnp.int32, (toks, keys), 1)
    bias = jnp.where(k_pos <= q_pos, 0.0, -1e30)
    bias = jnp.concatenate([bias] * per_group, axis=0)
    scaling = HEAD_DIM ** (-0.5)
    squares = jnp.zeros((toks, 1), F32)
    for g in range(kv_local):
        head = slice(g * HEAD_DIM, (g + 1) * HEAD_DIM)
        base = g * per_group * HEAD_DIM
        qs = jnp.concatenate(
            [
                q_ref[:, base + j * HEAD_DIM : base + (j + 1) * HEAD_DIM]
                for j in range(per_group)
            ],
            axis=0,
        )
        ks = kbuf[:, :, head].reshape(keys, HEAD_DIM)
        vs = vbuf[:, :, head].reshape(keys, HEAD_DIM)
        s = lax.dot_general(qs, ks, (((1,), (1,)), ((), ())), preferred_element_type=F32)
        s = s * scaling + bias
        m = jnp.max(s, axis=1, keepdims=True)
        p = jnp.exp(s - m)
        total = jnp.sum(p, axis=1, keepdims=True)
        att = jnp.dot(p.astype(BF16), vs, preferred_element_type=F32) / total
        for j in range(per_group):
            cols = slice(base + j * HEAD_DIM, base + (j + 1) * HEAD_DIM)
            h = (res_ref[:, cols].astype(F32) + att[j * toks : (j + 1) * toks]).astype(BF16)
            hid[:, cols] = h
            squares = squares + jnp.sum(jnp.square(h.astype(F32)), axis=1, keepdims=True)

    sq_send[...] = jnp.broadcast_to(squares, sq_send.shape)
    sq_copy = pltpu.make_async_remote_copy(
        src_ref=sq_send, dst_ref=sq_recv, send_sem=sq_sem.at[0], recv_sem=sq_sem.at[1],
        device_id={"exp": sib}, device_id_type=MESH,
    )
    sq_copy.start()
    my_feat = pl.multiple_of(x * half_feat, half_feat)
    sib_feat = pl.multiple_of(sib * half_feat, half_feat)
    gain = gain_ref[:, pl.ds(my_feat, half_feat)]
    scaled = hid[...].astype(F32)
    sq_copy.wait()
    inv = lax.rsqrt((squares + sq_recv[:, 0:1]) / (2 * half_feat) + 1e-05)
    normed = (scaled * inv * gain).astype(BF16)

    sent = jnp.dot(place[...], normed, preferred_element_type=F32)
    my_expert = lax.div(me, spread)

    def disp_copy(p, dst, block, src_expert, slot):
        return pltpu.make_async_remote_copy(
            src_ref=send_buf[p].at[src_expert], dst_ref=recv_own[p].at[block],
            send_sem=disp_send.at[p, slot], recv_sem=disp_recv.at[p, block],
            device_id={"ctx": dst}, device_id_type=MESH,
        )

    def sib_copy(p, src, block):
        return pltpu.make_async_remote_copy(
            src_ref=src, dst_ref=recv_sib[p].at[block],
            send_sem=sib_send.at[p, block], recv_sem=sib_recv.at[p, block],
            device_id={"exp": sib}, device_id_type=MESH,
        )

    def p_copy(p, j):
        return pltpu.make_async_remote_copy(
            src_ref=psend[p].at[j], dst_ref=precv[p].at[j],
            send_sem=p_send.at[p, j], recv_sem=p_recv.at[p, j],
            device_id={"exp": sib}, device_id_type=MESH,
        )

    def r_copy(p, j, dst, block, slot):
        return pltpu.make_async_remote_copy(
            src_ref=rsend[p].at[j, dst], dst_ref=rrecv[p].at[j, block],
            send_sem=r_send.at[p, j, slot], recv_sem=r_recv.at[p, j, block],
            device_id={"ctx": dst}, device_id_type=MESH,
        )

    start = 0
    for p, size in enumerate(PARTS):
        part = sent[start : start + EXPERTS * size]
        start += EXPERTS * size
        send_buf[p][...] = part.reshape(EXPERTS, size, half_feat).astype(BF16)
        for m in order:
            dst = flip(m)
            disp_copy(p, dst, me, lax.div(dst, spread), m).start()
        sib_copy(p, send_buf[p].at[my_expert], me).start()
        recv_own[p][me] = send_buf[p][my_expert]

    for p, size in enumerate(PARTS):
        rows = n * size
        for m in order:
            src = flip(m)
            disp_copy(p, src, src, my_expert, m).wait_recv()
            sib_copy(p, recv_own[p].at[src], src).start()

        flat[0:rows, :] = recv_own[p][...].astype(F32).reshape(rows, half_feat).astype(BF16)
        if p == 0:
            wg_copy.wait()
        for c in range(ff // 256):
            cols = slice(c * 256, (c + 1) * 256)
            acc[0:rows, cols] = jnp.dot(
                flat[0:rows, :], wg[pl.ds(my_feat, half_feat), cols],
                preferred_element_type=F32,
            )
        for m in (0,) + tuple(order):
            sib_copy(p, send_buf[p].at[0], flip(m)).wait_recv()
        flat[0:rows, :] = recv_sib[p][...].astype(F32).reshape(rows, half_feat).astype(BF16)
        for c in range(ff // 256):
            cols = slice(c * 256, (c + 1) * 256)
            v = acc[0:rows, cols] + jnp.dot(
                flat[0:rows, :], wg[pl.ds(sib_feat, half_feat), cols],
                preferred_element_type=F32,
            )
            act[0:rows, cols] = (v / (1.0 + jnp.exp(-v))).astype(BF16)

        if p == 0:
            wd_copy.wait()
        for j in range(chunks):
            cols = pl.ds(pl.multiple_of(sib_feat + j * CHUNK, 128), CHUNK)
            y = jnp.dot(act[0:rows, :], wd[:, cols], preferred_element_type=F32)
            psend[p][j] = y.reshape(n, size, CHUNK).astype(BF16)
            p_copy(p, j).start()
        for j in range(chunks):
            cols = pl.ds(pl.multiple_of(my_feat + j * CHUNK, 128), CHUNK)
            y = jnp.dot(act[0:rows, :], wd[:, cols], preferred_element_type=F32)
            p_copy(p, j).wait_recv()
            rsend[p][j] = (y.reshape(n, size, CHUNK) + precv[p][j].astype(F32)).astype(BF16)
            for m in order:
                r_copy(p, j, flip(m), me, m).start()
            rrecv[p][j, me] = rsend[p][j, me]

    start = 0
    for p, size in enumerate(PARTS):
        lines = EXPERTS * size
        comb_part = comb[start : start + lines, :]
        start += lines
        for j in range(chunks):
            for m in order:
                src = flip(m)
                r_copy(p, j, src, src, m).wait_recv()
            back = rrecv[p][j].astype(F32).reshape(EXPERTS, spread, size, CHUNK)
            if spread == 1:
                terms = [back.reshape(lines, CHUNK).astype(BF16)]
            else:
                back = jnp.sum(back, axis=1).reshape(lines, CHUNK)
                top = back.astype(BF16)
                terms = [top, (back - top.astype(F32)).astype(BF16)]
            cols = slice(j * CHUNK, (j + 1) * CHUNK)
            mixed = branch[:, cols] if p else None
            for term in terms:
                both = lax.dot_general(
                    comb_part, term, (((0,), (0,)), ((), ())), preferred_element_type=F32
                )
                both = both[:toks] + both[toks:]
                mixed = both if mixed is None else mixed + both
            branch[:, cols] = mixed

    @pl.when(parity == 0)
    def _():
        for c in own_copies(partner, 0):
            c.wait_send()

    for dz in range(1, nz):
        @pl.when(level + dz < nz)
        def _():
            for c in own_copies(me + 2 * dz, dz):
                c.wait_send()

        @pl.when(level - dz >= 0)
        def _():
            for c in relay_copies(me - 2 * dz, nz + dz - 1):
                c.wait_send()

    for p in range(len(PARTS)):
        for m in order:
            dst = flip(m)
            disp_copy(p, dst, me, lax.div(dst, spread), m).wait_send()
        for m in (0,) + tuple(order):
            sib_copy(p, send_buf[p].at[0], flip(m)).wait_send()
        for j in range(chunks):
            p_copy(p, j).wait_send()
            for m in order:
                r_copy(p, j, flip(m), me, m).wait_send()


def solution(mesh):
    n = mesh.shape["ctx"]

    def body(q, k, v, res, gain, ids, rw, w_gate, w_down):
        toks, half_feat = q.shape
        ff = w_gate.shape[1]
        slots = EXPERTS * CAP
        chunks = half_feat // CHUNK
        parts = len(PARTS)
        most = n * max(PARTS)
        dma = pltpu.SemaphoreType.DMA
        vmem = pl.BlockSpec(memory_space=pltpu.VMEM)
        anyspace = pl.BlockSpec(memory_space=pl.ANY)
        by_part = lambda f: [pltpu.VMEM(f(size), BF16) for size in PARTS]
        hidden, branch = pl.pallas_call(
            functools.partial(kernel, n),
            out_shape=(
                jax.ShapeDtypeStruct((toks, half_feat), BF16),
                jax.ShapeDtypeStruct((toks, half_feat), F32),
            ),
            in_specs=[vmem] * 7 + [anyspace] * 2,
            out_specs=(vmem, vmem),
            scratch_shapes=[
                pltpu.VMEM((n, toks, k.shape[1]), BF16),
                pltpu.VMEM((n, toks, k.shape[1]), BF16),
                pltpu.VMEM(w_gate.shape, BF16),
                pltpu.VMEM(w_down.shape, BF16),
                pltpu.VMEM((slots, toks), BF16),
                pltpu.VMEM((slots, 2 * toks), BF16),
                pltpu.VMEM((toks, 128), F32),
                pltpu.VMEM((toks, 128), F32),
            ]
            + by_part(lambda size: (EXPERTS, size, half_feat))
            + by_part(lambda size: (n, size, half_feat))
            + by_part(lambda size: (n, size, half_feat))
            + [
                pltpu.VMEM((most, ff), F32),
                pltpu.VMEM((most, ff), BF16),
                pltpu.VMEM((most, half_feat), BF16),
            ]
            + by_part(lambda size: (chunks, n, size, CHUNK))
            + by_part(lambda size: (chunks, n, size, CHUNK))
            + by_part(lambda size: (chunks, n, size, CHUNK))
            + by_part(lambda size: (chunks, n, size, CHUNK))
            + [
                dma((2,)),
                dma((2, n)),
                dma((2, n)),
                dma((2,)),
                dma((parts, n)),
                dma((parts, n)),
                dma((parts, n)),
                dma((parts, n)),
                dma((parts, chunks)),
                dma((parts, chunks)),
                dma((parts, chunks, n)),
                dma((parts, chunks, n)),
            ],
            compiler_params=pltpu.CompilerParams(
                collective_id=0, has_side_effects=True, vmem_limit_bytes=56 * 1024 * 1024
            ),
        )(q, k, v, res, gain.reshape(1, -1), ids.T, rw.T, w_gate, w_down)
        return (hidden.astype(F32) + branch).astype(BF16)

    rows_spec = P(("groups", "ctx"), "exp")
    in_specs = (
        rows_spec, rows_spec, rows_spec, rows_spec, P(),
        P(("groups", "ctx"), None), P(("groups", "ctx"), None),
        P(None, ("ctx", "exp")), P(("ctx", "exp"), None),
    )
    return jax.shard_map(
        body, mesh=mesh, in_specs=in_specs, out_specs=rows_spec, check_vma=False
    )
```

```python
import functools

import jax
import jax.numpy as jnp
from jax import lax
from jax.experimental import pallas as pl
from jax.experimental.pallas import tpu as pltpu
from jax.sharding import PartitionSpec as P

HEAD_DIM = 128
EXPERTS = 8
HALF_CAP = 12
CAP = 2 * HALF_CAP
PARTS = (8, 16)
CHUNK = 768
MESH = pl.DeviceIdType.MESH
F32 = jnp.float32
BF16 = jnp.bfloat16


def kernel(
    n,
    q_hbm, k_ref, v_ref, res_hbm, gain_hbm, ids_hbm, rw_hbm, wg_hbm, wd_hbm,
    out_ref,
    hid, branch, q_ref, res_ref, gain_ref, ids_ref, rw_ref, in_sem,
    kbuf, vbuf, wg, wd, place, comb, sq_send, sq_recv,
    send_a, send_b, own_a, own_b, other_a, other_b, acc, act, flat,
    psend_a, psend_b, precv_a, precv_b, rsend_a, rsend_b, rrecv_a, rrecv_b,
    w_sem, kv_send, kv_recv, sq_sem, disp_send, disp_recv, sib_send, sib_recv,
    p_send, p_recv, r_send, r_recv,
):
    send_buf, recv_own, recv_sib = (send_a, send_b), (own_a, own_b), (other_a, other_b)
    psend, precv = (psend_a, psend_b), (precv_a, precv_b)
    rsend, rrecv = (rsend_a, rsend_b), (rrecv_a, rrecv_b)
    me = lax.axis_index("ctx")
    x = lax.axis_index("exp")
    sib = 1 - x
    toks = q_ref.shape[0]
    half_feat = q_ref.shape[1]
    kv_local = k_ref.shape[1] // HEAD_DIM
    per_group = half_feat // HEAD_DIM // kv_local
    spread = n // EXPERTS
    slots = EXPERTS * CAP
    chunks = half_feat // CHUNK
    nz = n // 2
    ff = wg.shape[1]

    def flip(m):
        other, bit = me, 1
        while bit < n:
            if m & bit:
                other = other + bit * (1 - 2 * lax.rem(lax.div(me, bit), 2))
            bit *= 2
        return other

    order = range(1, n)

    wg_copy = pltpu.make_async_copy(wg_hbm, wg, w_sem.at[0])
    wd_copy = pltpu.make_async_copy(wd_hbm, wd, w_sem.at[1])
    loads = [
        pltpu.make_async_copy(src, dst, in_sem.at[i])
        for i, (src, dst) in enumerate(
            (
                (ids_hbm, ids_ref), (rw_hbm, rw_ref), (k_ref, kbuf.at[me]), (v_ref, vbuf.at[me]),
                (q_hbm, q_ref), (res_hbm, res_ref), (gain_hbm, gain_ref),
            )
        )
    ]
    for load in loads:
        load.start()
    wg_copy.start()
    wd_copy.start()

    barrier = pltpu.get_barrier_semaphore()
    for d in range(1, n):
        pl.semaphore_signal(
            barrier, inc=1, device_id={"ctx": lax.rem(me + d, n)}, device_id_type=MESH
        )
    pl.semaphore_signal(barrier, inc=1, device_id={"exp": sib}, device_id_type=MESH)
    pl.semaphore_wait(barrier, n)

    parity = lax.rem(me, 2)
    level = lax.div(me, 2)
    partner = me + 1 - 2 * parity
    bufs = (kbuf, vbuf)

    def kv_copy(i, src, block, dst, slot):
        return pltpu.make_async_remote_copy(
            src_ref=src,
            dst_ref=bufs[i].at[block],
            send_sem=kv_send.at[i, slot],
            recv_sem=kv_recv.at[i, block],
            device_id={"ctx": dst},
            device_id_type=MESH,
        )

    def own_copies(dst, slot):
        return [kv_copy(i, (k_ref, v_ref)[i], me, dst, slot) for i in range(2)]

    def relay_copies(block, slot):
        return [kv_copy(i, bufs[i].at[block], block, partner, slot) for i in range(2)]

    @pl.when(parity == 0)
    def _():
        for c in own_copies(partner, 0):
            c.start()

    for dz in range(1, nz):
        @pl.when(level + dz < nz)
        def _():
            for c in own_copies(me + 2 * dz, dz):
                c.start()

    for b in range(n):
        @pl.when(b > me)
        def _():
            kbuf[b] = jnp.zeros(k_ref.shape, BF16)
            vbuf[b] = jnp.zeros(v_ref.shape, BF16)

    row = lax.broadcasted_iota(jnp.int32, (slots, toks), 0)
    expert = jnp.zeros((slots, toks), jnp.int32)
    pos = row
    start, first_row = 0, 0
    for size in PARTS:
        for e in range(EXPERTS):
            here = row >= start + e * size
            expert = jnp.where(here, e, expert)
            pos = jnp.where(here, row - (start + e * size) + first_row, pos)
        start, first_row = start + EXPERTS * size, first_row + size
    token = lax.broadcasted_iota(jnp.int32, (slots, toks), 1)
    block_len = toks // 2
    in_second = (token >= block_len).astype(jnp.int32)
    loads[0].wait()
    loads[1].wait()
    ids = ids_ref[...]
    rw = rw_ref[...]
    first = jnp.where(ids[0:1, :] == expert, 1.0, 0.0)
    second = jnp.where(ids[1:2, :] == expert, 1.0, 0.0)
    chosen = first + second
    t_row = lax.broadcasted_iota(jnp.int32, (toks, toks), 0)
    t_col = lax.broadcasted_iota(jnp.int32, (toks, toks), 1)
    same = (t_row >= block_len) == (t_col >= block_len)
    upper = jnp.where(same & (t_row < t_col), 1.0, 0.0).astype(BF16)
    rank = jnp.dot(chosen.astype(BF16), upper, preferred_element_type=F32)
    wanted = (pos - in_second * HALF_CAP).astype(F32)
    placing = jnp.where(rank == wanted, chosen, 0.0)
    place[...] = placing.astype(BF16)
    weight = placing * (first * rw[0:1, :] + second * rw[1:2, :])
    high = weight.astype(BF16)
    comb[:, 0:toks] = high
    comb[:, toks:] = (weight - high.astype(F32)).astype(BF16)

    for dz in range(1, nz):
        @pl.when(level - dz >= 0)
        def _():
            block = me - 2 * dz
            for c in relay_copies(block, nz + dz - 1):
                c.wait_recv()
                c.start()
    for j in range(nz):
        block = 2 * j + 1 - parity

        @pl.when(block < me)
        def _():
            for c in relay_copies(block, 0):
                c.wait_recv()

    for load in loads[2:]:
        load.wait()
    keys = n * toks
    q_pos = me * toks + lax.broadcasted_iota(jnp.int32, (toks, keys), 0)
    k_pos = lax.broadcasted_iota(jnp.int32, (toks, keys), 1)
    bias = jnp.where(k_pos <= q_pos, 0.0, -1e30)
    bias = jnp.concatenate([bias] * per_group, axis=0)
    scaling = HEAD_DIM ** (-0.5)
    squares = jnp.zeros((toks, 1), F32)
    for g in range(kv_local):
        head = slice(g * HEAD_DIM, (g + 1) * HEAD_DIM)
        base = g * per_group * HEAD_DIM
        qs = jnp.concatenate(
            [
                q_ref[:, base + j * HEAD_DIM : base + (j + 1) * HEAD_DIM]
                for j in range(per_group)
            ],
            axis=0,
        )
        ks = kbuf[:, :, head].reshape(keys, HEAD_DIM)
        vs = vbuf[:, :, head].reshape(keys, HEAD_DIM)
        s = lax.dot_general(qs, ks, (((1,), (1,)), ((), ())), preferred_element_type=F32)
        s = s * scaling + bias
        m = jnp.max(s, axis=1, keepdims=True)
        p = jnp.exp(s - m)
        total = jnp.sum(p, axis=1, keepdims=True)
        att = jnp.dot(p.astype(BF16), vs, preferred_element_type=F32) / total
        for j in range(per_group):
            cols = slice(base + j * HEAD_DIM, base + (j + 1) * HEAD_DIM)
            h = (res_ref[:, cols].astype(F32) + att[j * toks : (j + 1) * toks]).astype(BF16)
            hid[:, cols] = h
            squares = squares + jnp.sum(jnp.square(h.astype(F32)), axis=1, keepdims=True)

    sq_send[...] = jnp.broadcast_to(squares, sq_send.shape)
    sq_copy = pltpu.make_async_remote_copy(
        src_ref=sq_send, dst_ref=sq_recv, send_sem=sq_sem.at[0], recv_sem=sq_sem.at[1],
        device_id={"exp": sib}, device_id_type=MESH,
    )
    sq_copy.start()
    my_feat = pl.multiple_of(x * half_feat, half_feat)
    sib_feat = pl.multiple_of(sib * half_feat, half_feat)
    gain = gain_ref[:, pl.ds(my_feat, half_feat)]
    scaled = hid[...].astype(F32)
    sq_copy.wait()
    inv = lax.rsqrt((squares + sq_recv[:, 0:1]) / (2 * half_feat) + 1e-05)
    normed = (scaled * inv * gain).astype(BF16)

    sent = jnp.dot(place[...], normed, preferred_element_type=F32)
    my_expert = lax.div(me, spread)

    def disp_copy(p, dst, block, src_expert, slot):
        return pltpu.make_async_remote_copy(
            src_ref=send_buf[p].at[src_expert], dst_ref=recv_own[p].at[block],
            send_sem=disp_send.at[p, slot], recv_sem=disp_recv.at[p, block],
            device_id={"ctx": dst}, device_id_type=MESH,
        )

    def sib_copy(p, src, block):
        return pltpu.make_async_remote_copy(
            src_ref=src, dst_ref=recv_sib[p].at[block],
            send_sem=sib_send.at[p, block], recv_sem=sib_recv.at[p, block],
            device_id={"exp": sib}, device_id_type=MESH,
        )

    def p_copy(p, j):
        return pltpu.make_async_remote_copy(
            src_ref=psend[p].at[j], dst_ref=precv[p].at[j],
            send_sem=p_send.at[p, j], recv_sem=p_recv.at[p, j],
            device_id={"exp": sib}, device_id_type=MESH,
        )

    def r_copy(p, j, dst, block, slot):
        return pltpu.make_async_remote_copy(
            src_ref=rsend[p].at[j, dst], dst_ref=rrecv[p].at[j, block],
            send_sem=r_send.at[p, j, slot], recv_sem=r_recv.at[p, j, block],
            device_id={"ctx": dst}, device_id_type=MESH,
        )

    start = 0
    for p, size in enumerate(PARTS):
        part = sent[start : start + EXPERTS * size]
        start += EXPERTS * size
        send_buf[p][...] = part.reshape(EXPERTS, size, half_feat).astype(BF16)
        for m in order:
            dst = flip(m)
            disp_copy(p, dst, me, lax.div(dst, spread), m).start()
        sib_copy(p, send_buf[p].at[my_expert], me).start()
        recv_own[p][me] = send_buf[p][my_expert]

    for p, size in enumerate(PARTS):
        rows = n * size
        for m in order:
            src = flip(m)
            disp_copy(p, src, src, my_expert, m).wait_recv()
            sib_copy(p, recv_own[p].at[src], src).start()

        flat[0:rows, :] = recv_own[p][...].astype(F32).reshape(rows, half_feat).astype(BF16)
        if p == 0:
            wg_copy.wait()
        for c in range(ff // 256):
            cols = slice(c * 256, (c + 1) * 256)
            acc[0:rows, cols] = jnp.dot(
                flat[0:rows, :], wg[pl.ds(my_feat, half_feat), cols],
                preferred_element_type=F32,
            )
        for m in (0,) + tuple(order):
            sib_copy(p, send_buf[p].at[0], flip(m)).wait_recv()
        flat[0:rows, :] = recv_sib[p][...].astype(F32).reshape(rows, half_feat).astype(BF16)
        for c in range(ff // 256):
            cols = slice(c * 256, (c + 1) * 256)
            v = acc[0:rows, cols] + jnp.dot(
                flat[0:rows, :], wg[pl.ds(sib_feat, half_feat), cols],
                preferred_element_type=F32,
            )
            act[0:rows, cols] = (v / (1.0 + jnp.exp(-v))).astype(BF16)

        if p == 0:
            wd_copy.wait()
        for j in range(chunks):
            cols = pl.ds(pl.multiple_of(sib_feat + j * CHUNK, 128), CHUNK)
            y = jnp.dot(act[0:rows, :], wd[:, cols], preferred_element_type=F32)
            psend[p][j] = y.reshape(n, size, CHUNK).astype(BF16)
            p_copy(p, j).start()
        for j in range(chunks):
            cols = pl.ds(pl.multiple_of(my_feat + j * CHUNK, 128), CHUNK)
            y = jnp.dot(act[0:rows, :], wd[:, cols], preferred_element_type=F32)
            p_copy(p, j).wait_recv()
            rsend[p][j] = (y.reshape(n, size, CHUNK) + precv[p][j].astype(F32)).astype(BF16)
            for m in order:
                r_copy(p, j, flip(m), me, m).start()
            rrecv[p][j, me] = rsend[p][j, me]

    start = 0
    for p, size in enumerate(PARTS):
        lines = EXPERTS * size
        comb_part = comb[start : start + lines, :]
        start += lines
        for j in range(chunks):
            for m in order:
                src = flip(m)
                r_copy(p, j, src, src, m).wait_recv()
            back = rrecv[p][j].astype(F32).reshape(EXPERTS, spread, size, CHUNK)
            if spread == 1:
                terms = [back.reshape(lines, CHUNK).astype(BF16)]
            else:
                back = jnp.sum(back, axis=1).reshape(lines, CHUNK)
                top = back.astype(BF16)
                terms = [top, (back - top.astype(F32)).astype(BF16)]
            cols = slice(j * CHUNK, (j + 1) * CHUNK)
            mixed = branch[:, cols] if p else None
            for term in terms:
                both = lax.dot_general(
                    comb_part, term, (((0,), (0,)), ((), ())), preferred_element_type=F32
                )
                both = both[:toks] + both[toks:]
                mixed = both if mixed is None else mixed + both
            if p < len(PARTS) - 1:
                branch[:, cols] = mixed
            else:
                out_ref[:, cols] = (hid[:, cols].astype(F32) + mixed).astype(BF16)

    @pl.when(parity == 0)
    def _():
        for c in own_copies(partner, 0):
            c.wait_send()

    for dz in range(1, nz):
        @pl.when(level + dz < nz)
        def _():
            for c in own_copies(me + 2 * dz, dz):
                c.wait_send()

        @pl.when(level - dz >= 0)
        def _():
            for c in relay_copies(me - 2 * dz, nz + dz - 1):
                c.wait_send()

    for p in range(len(PARTS)):
        for m in order:
            dst = flip(m)
            disp_copy(p, dst, me, lax.div(dst, spread), m).wait_send()
        for m in (0,) + tuple(order):
            sib_copy(p, send_buf[p].at[0], flip(m)).wait_send()
        for j in range(chunks):
            p_copy(p, j).wait_send()
            for m in order:
                r_copy(p, j, flip(m), me, m).wait_send()


def solution(mesh):
    n = mesh.shape["ctx"]

    def body(q, k, v, res, gain, ids, rw, w_gate, w_down):
        toks, half_feat = q.shape
        ff = w_gate.shape[1]
        slots = EXPERTS * CAP
        chunks = half_feat // CHUNK
        parts = len(PARTS)
        most = n * max(PARTS)
        dma = pltpu.SemaphoreType.DMA
        vmem = pl.BlockSpec(memory_space=pltpu.VMEM)
        by_part = lambda f: [pltpu.VMEM(f(size), BF16) for size in PARTS]
        return pl.pallas_call(
            functools.partial(kernel, n),
            out_shape=jax.ShapeDtypeStruct((toks, half_feat), BF16),
            in_specs=[pl.BlockSpec(memory_space=pltpu.HBM)] * 9,
            out_specs=vmem,
            scratch_shapes=[
                pltpu.VMEM(q.shape, BF16),
                pltpu.VMEM(q.shape, F32),
                pltpu.VMEM(q.shape, BF16),
                pltpu.VMEM(res.shape, BF16),
                pltpu.VMEM((1, gain.shape[0]), F32),
                pltpu.VMEM(ids.T.shape, jnp.int32),
                pltpu.VMEM(rw.T.shape, F32),
                dma((7,)),
                pltpu.VMEM((n, toks, k.shape[1]), BF16),
                pltpu.VMEM((n, toks, k.shape[1]), BF16),
                pltpu.VMEM(w_gate.shape, BF16),
                pltpu.VMEM(w_down.shape, BF16),
                pltpu.VMEM((slots, toks), BF16),
                pltpu.VMEM((slots, 2 * toks), BF16),
                pltpu.VMEM((toks, 128), F32),
                pltpu.VMEM((toks, 128), F32),
            ]
            + by_part(lambda size: (EXPERTS, size, half_feat))
            + by_part(lambda size: (n, size, half_feat))
            + by_part(lambda size: (n, size, half_feat))
            + [
                pltpu.VMEM((most, ff), F32),
                pltpu.VMEM((most, ff), BF16),
                pltpu.VMEM((most, half_feat), BF16),
            ]
            + by_part(lambda size: (chunks, n, size, CHUNK))
            + by_part(lambda size: (chunks, n, size, CHUNK))
            + by_part(lambda size: (chunks, n, size, CHUNK))
            + by_part(lambda size: (chunks, n, size, CHUNK))
            + [
                dma((2,)),
                dma((2, n)),
                dma((2, n)),
                dma((2,)),
                dma((parts, n)),
                dma((parts, n)),
                dma((parts, n)),
                dma((parts, n)),
                dma((parts, chunks)),
                dma((parts, chunks)),
                dma((parts, chunks, n)),
                dma((parts, chunks, n)),
            ],
            compiler_params=pltpu.CompilerParams(
                collective_id=0, has_side_effects=True, vmem_limit_bytes=56 * 1024 * 1024
            ),
        )(q, k, v, res, gain.reshape(1, -1), ids.T, rw.T, w_gate, w_down)

    rows_spec = P(("groups", "ctx"), "exp")
    in_specs = (
        rows_spec, rows_spec, rows_spec, rows_spec, P(),
        P(("groups", "ctx"), None), P(("groups", "ctx"), None),
        P(None, ("ctx", "exp")), P(("ctx", "exp"), None),
    )
    return jax.shard_map(
        body, mesh=mesh, in_specs=in_specs, out_specs=rows_spec, check_vma=False
    )
```
